32 devices in a mesh: fsdp: 2 (over core), ctx: 4 (over y, x), tp: 4 (over z).
Axes of the slice: x: 2, y: 2, z: 4, core: 2. Of those that a mesh axis runs over, the one named last changes fastest.
Arguments:
- inputs: bfloat16 [2, 1024, 1088], P('fsdp', 'ctx'), may hold values from -60 to 60
- segments: int32 [2, 1024], P('fsdp'), may hold values from 0 to 3, never falling along the last dimension, each value on 1 to 512 neighbouring positions
- in_projection: bfloat16 [1088, 3, 1280], P('fsdp', None, 'tp'), may hold values from -2 to 2
- out_projection: bfloat16 [1280, 1088], P('tp', 'fsdp'), may hold values from -2 to 2
- up_projection: bfloat16 [1088, 4352], P('fsdp', 'tp'), may hold values from -0.1875 to 0.1875
- down_projection: bfloat16 [4352, 1088], P('tp', 'fsdp'), may hold values from -0.09375 to 0.09375
- first_gain: bfloat16 [1088], P('fsdp'), may hold values from 0.5 to 1.5
- first_bias: bfloat16 [1088], P('fsdp'), may hold values from -2.5 to 2.5
- second_gain: bfloat16 [1088], P('fsdp'), may hold values from 0.5 to 1.5
- second_bias: bfloat16 [1088], P('fsdp'), may hold values from -2.5 to 2.5
- cotangent: bfloat16 [2, 1024, 1088], P('fsdp', 'ctx'), may hold values from -6 to 6
Outputs:
- output: float32 [2, 1024, 1088], P('fsdp', 'ctx', 'tp')
- inputs_gradient: float32 [2, 1024, 1088], P('fsdp', 'ctx', 'tp')
- in_gradient: float32 [1088, 3, 1280], P('fsdp', None, 'tp')
- out_gradient: float32 [1280, 1088], P('tp', 'fsdp')
- up_gradient: float32 [1088, 4352], P('fsdp', 'tp')
- down_gradient: float32 [4352, 1088], P('tp', 'fsdp')
- first_gain_gradient: float32 [1088], P('fsdp')
- first_bias_gradient: float32 [1088], P('fsdp')
- second_gain_gradient: float32 [1088], P('fsdp')
- second_bias_gradient: float32 [1088], P('fsdp')
The draws below stay inside these ranges and needn't reach their ends.
Inputs may be any that keep to these rules, and one draw needn't show every extreme that they name: `segments`: within a sequence the segment number never falls; a document spans 1 to 512 positions, and some document spans exactly 512.
All inputs are finite; a program needn't handle non-finite values.
Results may differ from the reference program's by a relative error of at most 0.03.
Values may be sent and summed in bfloat16 or wider, within the bound.
No kernel may reach another device: no remote copies, remote signals or barrier semaphores. Data moves between devices by JAX's collectives and lax.ppermute only.
A program may use at most 128 MiB of HBM per device.

```python
import math
import jax
import jax.numpy as jnp
import numpy as np
from jax import lax

D = 1088
HEADS = 17
HEAD = 64
FF = 4352
HEADS_PAD = 20
SEQ = 1024
DOCS = 4
SEQS = 2


def draw_inputs(key, part):
    base_key, scale_key = jax.random.split(key, 2)
    scales = jnp.exp(jax.random.uniform(scale_key, (SEQS, SEQ, 1), jnp.float32, 0.0, math.log(10.0)))
    random_part = jnp.clip(jax.random.normal(base_key, (SEQS, SEQ, D), jnp.float32), -6.0, 6.0)
    values = random_part * scales
    return jnp.clip(values, -60.0, 60.0).astype(jnp.bfloat16)


def draw_in_projection(key, part):
    first_key, second_key, third_key = jax.random.split(key, 3)
    spread = D ** (-0.5)
    layout = (D, HEADS_PAD, HEAD)
    query_part = jax.random.normal(first_key, layout, jnp.float32) * spread
    key_part = jax.random.normal(second_key, layout, jnp.float32) * spread
    value_part = jax.random.normal(third_key, layout, jnp.float32) * spread
    stacked = jnp.stack([query_part, key_part, value_part], axis=1).reshape(D, 3, HEADS_PAD * HEAD)
    return jnp.clip(stacked, -2.0, 2.0).astype(jnp.bfloat16)


def strengthened(drawn, own_key, source, target, parts, factor):
    owner, partner = [(jnp.arange(drawn.shape[axis_at]) // (drawn.shape[axis_at] // parts)).reshape([-1 if axis == axis_at else 1 for axis in range(drawn.ndim)]) for axis_at in (source, target)]
    chosen = jax.random.permutation(own_key, parts)[partner]
    strong = (owner == chosen) | (owner == (partner + parts // 2) % parts)
    return jnp.where(strong, factor * drawn, drawn)


def block_levels(rng, dims, pieces, low, high):
    factor_of, own = 1.0, jax.random.fold_in(rng, 6)
    for axis_at, parts in pieces:
        heights = jnp.exp(jax.random.uniform(jax.random.fold_in(own, axis_at), (parts,), jnp.float32, low / len(pieces), high / len(pieces)))
        factor_of = factor_of * jnp.repeat(heights, dims[axis_at] // parts).reshape([-1 if axis == axis_at else 1 for axis in range(len(dims))])
    return factor_of


def split_up(number_of, total, most, lean):
    weights = [(1 << 20) // math.isqrt(grade ** lean) + 1 for grade in range(2, number_of + 1)]
    spare, counts = total - most - (number_of - 1), [1] * (number_of - 1)
    while spare > 0:
        movable = [i for i in range(number_of - 1) if counts[i] < most]
        whole, budget = sum([weights[i] for i in movable]), spare
        for i in movable:
            more = min(most - counts[i], max(1, budget * weights[i] // whole), spare)
            counts[i] = counts[i] + more
            spare = spare - more
    return np.array([most] + counts)


def ragged_sizes(stream_key, amount, total, limit, slope):
    if amount == 2:
        one = jax.random.randint(stream_key, (), max(1, total - limit), min(limit, total - 1) + 1)
        return jnp.stack([one, total - one])
    lengths = jnp.asarray(split_up(amount, total, limit, slope), jnp.int32)
    pairs = (amount - 1) // 2
    giver, sink = lengths[1:1 + 2 * pairs:2], lengths[2:2 + 2 * pairs:2]
    slack = jnp.minimum(giver - 1, limit - sink)
    moved = jax.random.randint(jax.random.fold_in(stream_key, 1), (pairs,), 0, 1 << 20) % (slack + 1)
    lengths = lengths.at[1:1 + 2 * pairs:2].set(giver - moved).at[2:2 + 2 * pairs:2].set(sink + moved)
    return lengths[jax.random.permutation(jax.random.fold_in(stream_key, 2), amount)]


def scatter_about(rng, shape, scale, limit, shards=(), held_as=jnp.bfloat16):
    factor_of = block_levels(rng, shape, shards, -0.22, 0.18) if shards else 1.0
    values = jax.random.normal(rng, shape, jnp.float32) * scale * factor_of
    return jnp.minimum(jnp.maximum(values, -limit), limit).astype(held_as)


def bell_draw_with(stream_key, extent, scale, limit, cuts, heavy, dtype=jnp.bfloat16):
    values = scale * jax.random.normal(stream_key, extent, jnp.float32)
    if cuts:
        values = values * block_levels(stream_key, extent, cuts, -0.22, 0.18)
    return jnp.clip(strengthened(values, jax.random.fold_in(stream_key, 3), *heavy), -limit, limit).astype(dtype)


def setup_inputs(seed: int = 0) -> dict:
    streams_of = jax.random.split(jax.random.key(seed), 12)
    inputs = draw_inputs(jax.random.fold_in(streams_of[11], 71), 0)
    segments = jax.vmap(lambda own: jnp.searchsorted(jnp.cumsum(ragged_sizes(own, DOCS, SEQ, SEQ // 2, 0)), jnp.arange(SEQ), side="right"))(jax.random.split(streams_of[1], SEQS)).reshape((SEQS, SEQ)).astype(jnp.int32)
    in_projection = draw_in_projection(jax.random.fold_in(streams_of[11], 71), 0)
    out_projection = scatter_about(streams_of[3], (HEADS_PAD * HEAD, D), (max(4, HEADS * HEAD // 128)) ** -0.5, 2.0, ((0, 4), (1, 2)))
    up_projection = scatter_about(streams_of[4], (D, FF), D ** -0.5, 0.1875, ((0, 2), (1, 4)))
    down_projection = scatter_about(streams_of[5], (FF, D), FF ** -0.5, 0.09375, ((0, 4), (1, 2)))
    first_gain = jnp.clip(1.0 + 0.1 * jax.random.normal(streams_of[6], (D,), jnp.float32), 0.5, 1.5).astype(jnp.bfloat16)
    first_bias = scatter_about(streams_of[7], (D,), 0.5, 2.5, ((0, 2),))
    second_gain = jnp.clip(1.0 + 0.1 * jax.random.normal(streams_of[8], (D,), jnp.float32), 0.5, 1.5).astype(jnp.bfloat16)
    second_bias = scatter_about(streams_of[9], (D,), 0.5, 2.5, ((0, 2),))
    cotangent = bell_draw_with(streams_of[10], (SEQS, SEQ, D), 1.0, 6.0, ((0, 2), (1, 4)), (0, 2, 2, 2.0))
    return dict(inputs=inputs, segments=segments, in_projection=in_projection, out_projection=out_projection, up_projection=up_projection, down_projection=down_projection, first_gain=first_gain, first_bias=first_bias, second_gain=second_gain, second_bias=second_bias, cotangent=cotangent)


EPSILON = 1e-05
NEGATIVE = -1e+30

def narrow(values):
    return lax.optimization_barrier(values.astype(jnp.bfloat16))

def normalize(values, gain_row, bias_row):
    center = values - lax.optimization_barrier(jnp.mean(values, axis=-1, keepdims=True))
    inverse = lax.rsqrt(lax.optimization_barrier(jnp.mean(center * center, axis=-1, keepdims=True)) + EPSILON)
    scaled = center * inverse
    return (scaled * gain_row.astype(jnp.float32) + bias_row.astype(jnp.float32), scaled, inverse)

def normalize_back(upstream, scaled, inverse, gain_row):
    weighted = upstream * gain_row.astype(jnp.float32)
    first_mean = lax.optimization_barrier(jnp.mean(weighted, axis=-1, keepdims=True))
    second_mean = lax.optimization_barrier(jnp.mean(weighted * scaled, axis=-1, keepdims=True))
    return inverse * (weighted - first_mean - scaled * second_mean)

def gelu_back(before, upstream):
    _, pullback = jax.vjp(lambda argument: jax.nn.gelu(argument, approximate=True), before)
    return pullback(upstream)[0]

def reference(inputs, segments, in_projection, out_projection, up_projection, down_projection, first_gain, first_bias, second_gain, second_bias, cotangent):
    inner_width = HEADS_PAD * HEAD
    score_scale = HEAD ** (-0.5)
    qkv_matrix = in_projection.reshape(D, 3 * inner_width)
    head_mask = (jnp.arange(HEADS_PAD) < HEADS).astype(jnp.float32)
    positions = jnp.arange(SEQ)
    causal = positions[None, :] <= positions[:, None]

    def one_sequence(totals, entries):
        sequence, labels, upstream = entries
        flat_inputs = sequence.astype(jnp.float32)
        normed_one, scaled_one, inverse_one = normalize(flat_inputs, first_gain, first_bias)
        normed_one = narrow(normed_one)
        projected = narrow(jnp.dot(normed_one, qkv_matrix, preferred_element_type=jnp.float32))
        projected = projected.astype(jnp.float32).reshape(SEQ, 3, HEADS_PAD, HEAD)
        queries = projected[:, 0]
        key_heads = projected[:, 1]
        values = projected[:, 2]
        allowed = (causal & (labels[None, :] == labels[:, None]))[None]
        scores = jnp.einsum('qhe,khe->hqk', queries, key_heads) * score_scale
        masked = jnp.where(allowed, scores, NEGATIVE)
        row_max = lax.optimization_barrier(jnp.max(masked, axis=-1, keepdims=True))
        row_total = lax.optimization_barrier(jnp.sum(jnp.where(allowed, jnp.exp(masked - row_max), 0.0), axis=-1, keepdims=True))
        log_total = row_max + jnp.log(row_total)
        weights_full = jnp.where(allowed, jnp.exp(masked - log_total), 0.0)
        weights_low = narrow(weights_full).astype(jnp.float32)
        attended = jnp.einsum('hqk,khe->qhe', weights_low, values) * head_mask[None, :, None]
        attended_low = narrow(attended)
        residual = flat_inputs + jnp.dot(attended_low.reshape(SEQ, inner_width), out_projection, preferred_element_type=jnp.float32)
        normed_two, scaled_two, inverse_two = normalize(residual, second_gain, second_bias)
        normed_two = narrow(normed_two)
        before = jnp.dot(normed_two, up_projection, preferred_element_type=jnp.float32)
        activated = narrow(jax.nn.gelu(before, approximate=True))
        output = residual + jnp.dot(activated, down_projection, preferred_element_type=jnp.float32)
        down_term = jnp.dot(activated.T, upstream, preferred_element_type=jnp.float32)
        before_gradient = narrow(gelu_back(before, jnp.dot(upstream, down_projection.T, preferred_element_type=jnp.float32)))
        up_term = jnp.dot(normed_two.T, before_gradient, preferred_element_type=jnp.float32)
        second_normed_gradient = jnp.dot(before_gradient, up_projection.T, preferred_element_type=jnp.float32)
        second_gain_term = lax.optimization_barrier(jnp.sum(second_normed_gradient * scaled_two, axis=0))
        second_bias_term = lax.optimization_barrier(jnp.sum(second_normed_gradient, axis=0))
        residual_gradient = upstream.astype(jnp.float32) + normalize_back(second_normed_gradient, scaled_two, inverse_two, second_gain)
        residual_low = narrow(residual_gradient)
        out_term = jnp.dot(attended_low.reshape(SEQ, inner_width).T, residual_low, preferred_element_type=jnp.float32)
        attended_gradient = jnp.dot(residual_low, out_projection.T, preferred_element_type=jnp.float32).reshape(SEQ, HEADS_PAD, HEAD)
        attended_gradient = narrow(attended_gradient * head_mask[None, :, None]).astype(jnp.float32)
        row_delta = lax.optimization_barrier(jnp.sum(attended_gradient * attended_low.astype(jnp.float32), axis=-1)).T
        weights_gradient = jnp.einsum('qhe,khe->hqk', attended_gradient, values)
        scores_gradient = narrow(weights_full * (weights_gradient - row_delta[:, :, None])).astype(jnp.float32)
        query_gradient = jnp.einsum('hqk,khe->qhe', scores_gradient, key_heads) * score_scale
        key_gradient = jnp.einsum('hqk,qhe->khe', scores_gradient, queries) * score_scale
        value_gradient = jnp.einsum('hqk,qhe->khe', weights_low, attended_gradient)
        qkv_gradient = narrow(jnp.stack([query_gradient, key_gradient, value_gradient], axis=1).reshape(SEQ, 3 * inner_width))
        in_term = jnp.dot(normed_one.T, qkv_gradient, preferred_element_type=jnp.float32).reshape(D, 3, inner_width)
        first_normed_gradient = jnp.dot(qkv_gradient, qkv_matrix.T, preferred_element_type=jnp.float32)
        first_gain_term = lax.optimization_barrier(jnp.sum(first_normed_gradient * scaled_one, axis=0))
        first_bias_term = lax.optimization_barrier(jnp.sum(first_normed_gradient, axis=0))
        inputs_gradient = residual_gradient + normalize_back(first_normed_gradient, scaled_one, inverse_one, first_gain)
        terms = (in_term, out_term, up_term, down_term, first_gain_term, first_bias_term, second_gain_term, second_bias_term)
        updated = tuple((running + addition for running, addition in zip(totals, terms)))
        return (updated, (output, inputs_gradient))
    starting = (jnp.zeros((D, 3, inner_width), jnp.float32), jnp.zeros((inner_width, D), jnp.float32), jnp.zeros((D, FF), jnp.float32), jnp.zeros((FF, D), jnp.float32), jnp.zeros((D,), jnp.float32), jnp.zeros((D,), jnp.float32), jnp.zeros((D,), jnp.float32), jnp.zeros((D,), jnp.float32))
    totals, (outputs, gradients) = lax.scan(one_sequence, starting, (inputs, segments, cotangent))
    return (outputs, gradients, totals[0], totals[1], totals[2], totals[3], totals[4], totals[5], totals[6], totals[7])
```

```python
import jax
import jax.numpy as jnp
from jax import lax
from jax.sharding import PartitionSpec as P

HEADS = 17
HEAD = 64
MAX_SPAN = 512

EPSILON = 1e-05
NEGATIVE = -1e30


f32 = jnp.float32
bf16 = jnp.bfloat16


def mm(a, b, dims):
    return lax.dot_general(a, b, (dims, ((), ())), preferred_element_type=f32)


def nn(a, b):
    return mm(a, b, ((1,), (0,)))


def tn(a, b):
    return mm(a, b, ((0,), (0,)))


def nt(a, b):
    return mm(a, b, ((1,), (1,)))


def take_rows(array, start, count):
    return lax.dynamic_slice_in_dim(array, start, count, 0)


def shift(size, step):
    return [(i, (i + step) % size) for i in range(size)]


def gelu_parts(before):
    activated, pullback = jax.vjp(lambda v: jax.nn.gelu(v, approximate=True), before)
    return activated, pullback(jnp.ones_like(before))[0]


def on_device(
    inputs,
    segments,
    in_projection,
    out_projection,
    up_projection,
    down_projection,
    first_gain,
    first_bias,
    second_gain,
    second_bias,
    cotangent,
):
    seqs_local, rows, width = inputs.shape
    inner = out_projection.shape[0]
    heads_local = inner // HEAD
    length = segments.shape[1]
    score_scale = HEAD ** (-0.5)
    tp_size = lax.axis_size("tp")
    ctx_size = lax.axis_size("ctx")
    fsdp_size = lax.axis_size("fsdp")
    tp_at = lax.axis_index("tp")
    ctx_at = lax.axis_index("ctx")
    paired = fsdp_size == 2
    own_half = lax.axis_index("fsdp") if paired else 0
    tokens = seqs_local * rows
    share = width // tp_size
    half = width // 2 if paired else width
    turn = own_half * half
    share_at = lax.rem(tp_at * share + turn, width) if paired else tp_at * share

    def swap(array):
        return lax.ppermute(array, "fsdp", [(0, 1), (1, 0)])

    def turned(array):
        if not paired:
            return array
        return jnp.concatenate(
            [take_rows(array, turn, half), take_rows(array, half - turn, half)], 0
        )

    def gather_parts(array, axis):
        if paired:
            return [array, swap(array)]
        return [lax.all_gather(array, "fsdp", axis=axis, tiled=True)]

    def wide(parts, axis):
        return jnp.concatenate(parts, axis) if len(parts) > 1 else parts[0]

    def tp_gather(piece):
        return [(tp_at, piece)] + [
            (lax.rem(tp_at + tp_size - k, tp_size), lax.ppermute(piece, "tp", shift(tp_size, k)))
            for k in range(1, tp_size)
        ]

    def tp_sum(piece):
        total = piece
        for k in range(1, tp_size):
            total = total + lax.ppermute(piece, "tp", shift(tp_size, k))
        return total

    def tp_scatter_sum(partial_value):
        low = partial_value.astype(bf16)
        total = None
        for k in range(1, tp_size):
            start = lax.rem(share_at + k * share, width)
            got = lax.ppermute(take_rows(low, start, share), "tp", shift(tp_size, k)).astype(f32)
            total = got if total is None else total + got
        return take_rows(partial_value, share_at, share) + total

    def tp_rows(piece):
        whole = jnp.zeros((width,) + piece.shape[1:], piece.dtype)
        for index, got in tp_gather(piece):
            start = lax.rem(index * share + turn, width) if paired else index * share
            whole = lax.dynamic_update_slice_in_dim(whole, got, start, 0)
        return whole

    cross = ctx_size == 4
    x_at, y_at = lax.rem(ctx_at, 2), ctx_at // 2
    pairs = {"x": [(0, 1), (1, 0), (2, 3), (3, 2)], "y": [(0, 2), (2, 0), (1, 3), (3, 1)]}
    at = {"x": x_at, "y": y_at}

    def ctx_step(value, low, axis):
        count = value.shape[0] // 2
        got = lax.ppermute(take_rows(low, (1 - at[axis]) * count, count), "ctx", pairs[axis])
        return take_rows(value, at[axis] * count, count) + got.astype(f32)

    def ctx_join(low, axis):
        got = lax.ppermute(low, "ctx", pairs[axis])
        first = at[axis] == 0
        return jnp.concatenate([jnp.where(first, low, got), jnp.where(first, got, low)], 0)

    def ctx_total(value, first, second):
        value = ctx_step(value, value.astype(bf16), first)
        value = ctx_step(value, value.astype(bf16), second)
        low = ctx_join(value.astype(bf16), second)
        return ctx_join(low, first)

    def ctx_sum(value, order="xy"):
        if not cross:
            return lax.psum(value.astype(bf16), "ctx").astype(f32)
        return ctx_total(value, order[0], order[1]).astype(f32)

    def ctx_sum_split(value):
        if not cross:
            return ctx_sum(value)
        count = value.shape[0] // 2
        return jnp.concatenate([ctx_sum(value[:count], "xy"), ctx_sum(value[count:], "yx")], 0)

    def ctx_sum_small(value):
        if not cross:
            return lax.psum(value, "ctx")
        value = value + lax.ppermute(value, "ctx", pairs["x"])
        return value + lax.ppermute(value, "ctx", pairs["y"])

    x_low = turned(inputs.reshape(tokens, width).T)
    upstream = turned(cotangent.reshape(tokens, width).T)
    in_parts = gather_parts(jnp.transpose(in_projection, (1, 2, 0)).reshape(3 * inner, -1), 1)
    vectors = jnp.stack([first_gain, first_bias, second_gain, second_bias]).astype(f32)
    vectors = wide(gather_parts(vectors, 1), 1)
    gain_one, bias_one, gain_two, bias_two = [vectors[i][:, None] for i in range(4)]
    out_parts = gather_parts(out_projection, 1)
    up_parts = gather_parts(up_projection, 0)
    down_parts = gather_parts(down_projection.T, 0)
    in_all, out_own = wide(in_parts, 1), wide(out_parts, 1)
    up_all, down_all = wide(up_parts, 0), wide(down_parts, 0)
    live = (
        tp_at * heads_local + jnp.arange(heads_local, dtype=jnp.int32) < HEADS
    ).astype(f32)[:, None, None]

    def normalize(values):
        center = values - jnp.mean(values, axis=0, keepdims=True)
        inverse = lax.rsqrt(jnp.mean(center * center, axis=0, keepdims=True) + EPSILON)
        return center * inverse, inverse

    def normalize_back(inverse, weighted, scaled, first_mean, second_mean):
        return inverse * (weighted - first_mean - scaled * second_mean)

    x = x_low.astype(f32)
    scaled_one, inverse_one = normalize(x)
    normed_one = (scaled_one * gain_one + bias_one).astype(bf16)
    projected = nn(in_all, normed_one).astype(bf16)

    back = min(ctx_size - 1, -(-(MAX_SPAN - 1) // rows))
    key_values = projected[inner:]
    blocks = [
        lax.ppermute(key_values, "ctx", [(i, i + k) for i in range(ctx_size - k)])
        for k in range(back, 0, -1)
    ] + [key_values]

    def by_head(array):
        return array.reshape(heads_local, HEAD, seqs_local, rows).transpose(2, 0, 1, 3)

    queries = by_head(projected[:inner])
    keys = jnp.concatenate([by_head(b[:inner]) for b in blocks], -1)
    values = jnp.concatenate([by_head(b[inner:]) for b in blocks], -1)
    span = keys.shape[-1]
    query_positions = ctx_at * rows + jnp.arange(rows, dtype=jnp.int32)
    key_positions = (ctx_at - back) * rows + jnp.arange(span, dtype=jnp.int32)
    padded = jnp.pad(segments, ((0, 0), (back * rows, 0)), constant_values=-1)
    key_labels = lax.dynamic_slice_in_dim(padded, ctx_at * rows, span, 1)
    query_labels = lax.dynamic_slice_in_dim(segments, ctx_at * rows, rows, 1)
    allowed = (
        (key_positions[None, :, None] <= query_positions[None, None, :])
        & (key_positions[None, :, None] >= 0)
        & (key_labels[:, :, None] == query_labels[:, None, :])
    )[:, None]

    def einsum(spec, a, b):
        return jnp.einsum(spec, a, b, preferred_element_type=f32)

    scores = einsum("shek,sheq->shkq", keys, queries) * score_scale
    masked = jnp.where(allowed, scores, NEGATIVE)
    row_max = jnp.max(masked, axis=2, keepdims=True)
    piece = jnp.where(allowed, jnp.exp(masked - row_max), 0.0)
    row_sum = jnp.sum(piece, axis=2, keepdims=True)
    weights_full = piece * (1.0 / row_sum)
    weights_low = weights_full.astype(bf16)
    attended = (einsum("shek,shkq->sheq", values, weights_low) * live).astype(bf16)
    flat_attended = attended.transpose(1, 2, 0, 3).reshape(inner, tokens)

    residual = x
    for (_, got), (_, matrix) in zip(tp_gather(flat_attended), tp_gather(out_own)):
        residual = residual + tn(matrix, got)
    scaled_two, inverse_two = normalize(residual)
    normed_two = (scaled_two * gain_two + bias_two).astype(bf16)

    act_gradient = tn(down_all, upstream)
    before = tn(up_all, normed_two)
    gelu_value, gelu_slope = gelu_parts(before)
    activated = gelu_value.astype(bf16)
    before_gradient = (gelu_slope * act_gradient).astype(bf16)
    second_partial = nn(up_all, before_gradient)
    second_share = tp_scatter_sum(second_partial)
    second_normed_gradient = tp_rows(second_share.astype(bf16)).astype(f32)
    forward_part = nn(down_all, activated)
    output_share = take_rows(residual, share_at, share) + tp_scatter_sum(forward_part)

    def weight_gradient(left, right, left_is_model):
        if paired:
            model = left if left_is_model else right
            other = right if left_is_model else left
            got_model, got_other = swap(model[half:]), swap(other)
            pieces = [(model[:half], other), (got_model, got_other)]
            pieces = [(m, o) if left_is_model else (o, m) for m, o in pieces]
            return sum(nt(a, b) for a, b in pieces)
        whole = nt(left, right)
        return lax.psum_scatter(
            whole.astype(bf16), "fsdp", scatter_dimension=0 if left_is_model else 1, tiled=True
        ).astype(f32)

    down_gradient = ctx_sum(weight_gradient(upstream, activated, True), "xy")
    up_gradient = ctx_sum(weight_gradient(normed_two, before_gradient, True), "yx")

    weighted_two = second_normed_gradient * gain_two
    residual_gradient = upstream.astype(f32) + normalize_back(
        inverse_two,
        weighted_two,
        scaled_two,
        jnp.mean(weighted_two, axis=0, keepdims=True),
        jnp.mean(weighted_two * scaled_two, axis=0, keepdims=True),
    )
    residual_low = residual_gradient.astype(bf16)
    out_gradient = ctx_sum_split(weight_gradient(flat_attended, residual_low, False))
    attended_gradient = nn(out_own, residual_low).reshape(heads_local, HEAD, seqs_local, rows)
    attended_gradient = (attended_gradient.transpose(2, 0, 1, 3) * live).astype(bf16)
    row_delta = jnp.sum(
        attended_gradient.astype(f32) * attended.astype(f32), axis=2, keepdims=True
    )
    weights_gradient = einsum("shek,sheq->shkq", values, attended_gradient)
    scores_gradient = (weights_full * (weights_gradient - row_delta)).astype(bf16)
    query_gradient = einsum("shek,shkq->sheq", keys, scores_gradient) * score_scale
    key_term = einsum("sheq,shkq->shek", queries, scores_gradient) * score_scale
    value_term = einsum("sheq,shkq->shek", attended_gradient, weights_low)

    def flat(array):
        return array.transpose(1, 2, 0, 3).reshape(inner, tokens)

    def block_of(index):
        return jnp.concatenate(
            [
                flat(term[..., index * rows : (index + 1) * rows])
                for term in (key_term, value_term)
            ],
            0,
        )

    key_value_gradient = block_of(back)
    for k in range(1, back + 1):
        sent = block_of(back - k).astype(bf16)
        got = lax.ppermute(sent, "ctx", [(i + k, i) for i in range(ctx_size - k)])
        key_value_gradient = key_value_gradient + got.astype(f32)
    combined = jnp.concatenate([flat(query_gradient), key_value_gradient], 0).astype(bf16)

    first_partial = tn(in_all, combined)
    weighted_part = first_partial * gain_one
    sums = tp_sum(
        jnp.concatenate(
            [
                jnp.sum(weighted_part, axis=0, keepdims=True),
                jnp.sum(weighted_part * scaled_one, axis=0, keepdims=True),
            ],
            0,
        )
    )
    first_share = tp_scatter_sum(first_partial)
    in_gradient = ctx_sum_split(weight_gradient(combined, normed_one, False))
    inputs_share = take_rows(residual_gradient, share_at, share) + normalize_back(
        inverse_one,
        first_share * take_rows(gain_one, share_at, share),
        take_rows(scaled_one, share_at, share),
        sums[0:1] / width,
        sums[1:2] / width,
    )

    def vector_sums(gradient, scaled):
        both = jnp.stack([jnp.sum(gradient * scaled, axis=1), jnp.sum(gradient, axis=1)])
        if paired:
            return both[:, :half] + swap(both[:, half:])
        return lax.psum_scatter(both, "fsdp", scatter_dimension=1, tiled=True)

    first_vectors = ctx_sum_small(tp_sum(vector_sums(first_partial, scaled_one)))
    second_vectors = ctx_sum_small(vector_sums(second_normed_gradient, scaled_two))

    def share_out(array):
        return array.T.reshape(seqs_local, rows, share)

    return (
        share_out(output_share),
        share_out(inputs_share),
        in_gradient.reshape(3, inner, -1).transpose(2, 0, 1),
        out_gradient,
        up_gradient,
        down_gradient.T,
        first_vectors[0],
        first_vectors[1],
        second_vectors[0],
        second_vectors[1],
    )


def solution(mesh):
    placed = (
        P("fsdp", "ctx", None),
        P("fsdp", None),
        P("fsdp", None, "tp"),
        P("tp", "fsdp"),
        P("fsdp", "tp"),
        P("tp", "fsdp"),
        P("fsdp"),
        P("fsdp"),
        P("fsdp"),
        P("fsdp"),
        P("fsdp", "ctx", None),
    )
    return jax.shard_map(
        on_device,
        mesh=mesh,
        in_specs=placed,
        out_specs=(
            P("fsdp", "ctx", "tp"),
            P("fsdp", "ctx", "tp"),
            P("fsdp", None, "tp"),
            P("tp", "fsdp"),
            P("fsdp", "tp"),
            P("tp", "fsdp"),
            P("fsdp"),
            P("fsdp"),
            P("fsdp"),
            P("fsdp"),
        ),
        check_vma=False,
    )
```

```python
import jax
import jax.numpy as jnp
from jax import lax
from jax.experimental import pallas as pl
from jax.experimental.pallas import tpu as pltpu
from jax.sharding import PartitionSpec as P

HEADS = 17
HEAD = 64
MAX_SPAN = 512

EPSILON = 1e-05
NEGATIVE = -1e30


f32 = jnp.float32
bf16 = jnp.bfloat16


def mm(a, b, dims):
    return lax.dot_general(a, b, (dims, ((), ())), preferred_element_type=f32)


def nn(a, b):
    return mm(a, b, ((1,), (0,)))


def tn(a, b):
    return mm(a, b, ((0,), (0,)))


def nt(a, b):
    return mm(a, b, ((1,), (1,)))


def take_rows(array, start, count):
    return lax.dynamic_slice_in_dim(array, start, count, 0)


def shift(size, step):
    return [(i, (i + step) % size) for i in range(size)]


def aligned(offset):
    return pl.multiple_of(offset, 16)


def call(kernel, outs, *operands, flops=0, name=None):
    moved = sum(a.size * a.dtype.itemsize for a in operands)
    return pl.pallas_call(
        kernel,
        out_shape=[jax.ShapeDtypeStruct(shape, dtype) for shape, dtype in outs],
        compiler_params=pltpu.CompilerParams(vmem_limit_bytes=36 << 20),
        cost_estimate=pl.CostEstimate(flops=int(flops), bytes_accessed=moved, transcendentals=0),
        name=name,
    )(*operands)


def half_offsets(paired, half):
    if not paired:
        return [0]
    own = lax.axis_index("fsdp")
    return [aligned(own * half), aligned((1 - own) * half)]


def tiles(total, step):
    return [(i, min(step, total - i)) for i in range(0, total, step)]


def norm_stats(value):
    mean = jnp.mean(value, axis=0, keepdims=True)
    center = value - mean
    inverse = lax.rsqrt(jnp.mean(center * center, axis=0, keepdims=True) + EPSILON)
    return mean, inverse


def put_rows(ref, rows):
    for i, row in enumerate(rows):
        ref[i : i + 1, :] = row


def gelu_parts(v):
    c = 0.7978845608028654
    inner = v * (c + (c * 0.044715) * v * v)
    t = jnp.tanh(inner)
    value = 0.5 * v * (1.0 + t)
    slope = 0.5 * (1.0 + t) + 0.5 * v * (1.0 - t * t) * (c + (3.0 * c * 0.044715) * v * v)
    return value, slope


def spread_chunks(refs, source, share, size):
    at = lax.axis_index("tp")
    for k, ref in enumerate(refs):
        start = aligned(lax.rem(at + k, size) * share)
        ref[...] = source[pl.ds(start, share), :].astype(ref.dtype)


def on_device(
    inputs,
    segments,
    in_projection,
    out_projection,
    up_projection,
    down_projection,
    first_gain,
    first_bias,
    second_gain,
    second_bias,
    cotangent,
):
    seqs_local, rows, width = inputs.shape
    inner = out_projection.shape[0]
    heads_local = inner // HEAD
    score_scale = HEAD ** (-0.5)
    tp_size = lax.axis_size("tp")
    ctx_size = lax.axis_size("ctx")
    fsdp_size = lax.axis_size("fsdp")
    tp_at = lax.axis_index("tp")
    ctx_at = lax.axis_index("ctx")
    paired = fsdp_size == 2
    own_half = lax.axis_index("fsdp") if paired else 0
    assert seqs_local == 1
    share = width // tp_size
    half = width // 2 if paired else width
    own_at = own_half * half
    share_at = tp_at * share

    def swap(array):
        return lax.ppermute(array, "fsdp", [(0, 1), (1, 0)])

    def gather_parts(array, axis):
        if paired:
            return [array, swap(array)]
        return [lax.all_gather(array, "fsdp", axis=axis, tiled=True)]

    def in_order(array):
        parts = gather_parts(array, 0)
        if not paired:
            return parts[0]
        first = own_half == 0
        return jnp.concatenate([jnp.where(first, *parts), jnp.where(first, *parts[::-1])])

    def tp_gather(piece):
        return [(tp_at, piece)] + [
            (lax.rem(tp_at + tp_size - k, tp_size), lax.ppermute(piece, "tp", shift(tp_size, k)))
            for k in range(1, tp_size)
        ]

    def tp_sum(piece):
        total = piece
        for k in range(1, tp_size):
            total = total + lax.ppermute(piece, "tp", shift(tp_size, k))
        return total

    def tp_send(chunks):
        return [
            lax.ppermute(chunk, "tp", shift(tp_size, k)) for k, chunk in enumerate(chunks, 1)
        ]

    def add_up(own, received):
        return sum((got.astype(f32) for got in received), own.astype(f32))

    cross = ctx_size == 4
    x_at, y_at = lax.rem(ctx_at, 2), ctx_at // 2
    pairs = {"x": [(0, 1), (1, 0), (2, 3), (3, 2)], "y": [(0, 2), (2, 0), (1, 3), (3, 1)]}
    at = {"x": x_at, "y": y_at}

    def ctx_send(value, axis):
        return lax.ppermute(value, "ctx", pairs[axis])

    def ctx_reduce(value, axis):
        count = value.shape[0] // 2
        got = ctx_send(take_rows(value, (1 - at[axis]) * count, count), axis)
        own = take_rows(value, at[axis] * count, count)
        return (own.astype(f32) + got.astype(f32)).astype(bf16)

    def ctx_join(low, axis):
        got = ctx_send(low, axis)
        first = at[axis] == 0
        return jnp.concatenate([jnp.where(first, low, got), jnp.where(first, got, low)], 0)

    def ctx_sum_pair(one, two):
        if not cross:
            return lax.psum((one, two), "ctx")
        one, two = ctx_reduce(one, "x"), ctx_reduce(two, "y")
        one, two = ctx_reduce(one, "y"), ctx_reduce(two, "x")
        one, two = ctx_join(one, "y"), ctx_join(two, "x")
        return ctx_join(one, "x"), ctx_join(two, "y")

    def ctx_sum_small(value):
        if not cross:
            return lax.psum(value, "ctx")
        value = value + ctx_send(value, "x")
        return value + ctx_send(value, "y")

    back = min(ctx_size - 1, -(-(MAX_SPAN - 1) // rows))
    span = (back + 1) * rows
    before_rows = back * rows
    raw = inputs[0].T
    raw_blocks = [
        lax.ppermute(raw, "ctx", [(i, i + k) for i in range(ctx_size - k)])
        for k in range(back, 0, -1)
    ]
    in_parts = gather_parts(jnp.transpose(in_projection, (1, 2, 0)).reshape(3 * inner, -1), 1)
    vectors = [in_order(v) for v in (first_gain, first_bias, second_gain, second_bias)]
    columns = jnp.stack(vectors, 1).astype(f32)
    out_rows = [piece for _, piece in tp_gather(out_projection)]
    up_parts = gather_parts(up_projection, 0)
    down_parts = gather_parts(down_projection.T, 0)
    upstream = cotangent[0].T
    hidden = up_projection.shape[1]
    n_parts = len(in_parts)
    ends = [rows * (i + 1) for i in range(back + 1)]

    key_labels = lax.dynamic_slice_in_dim(
        jnp.pad(segments[0], (before_rows, 0), constant_values=-1), ctx_at * rows, span, 0
    )[:, None]
    query_labels = lax.dynamic_slice_in_dim(segments, ctx_at * rows, rows, 1)

    def first_kernel(x_ref, col_ref, *refs):
        w_refs, (normed_ref, stats_ref, q_ref, kv_ref) = refs[:n_parts], refs[n_parts:]
        value = x_ref[...].astype(f32)
        mean, inverse = norm_stats(value)
        put_rows(stats_ref, [mean, inverse])
        normed = (value - mean) * inverse * col_ref[:, 0:1] + col_ref[:, 1:2]
        normed_ref[...] = normed.astype(bf16)
        offsets = half_offsets(paired, half)
        for start, count in tiles(3 * inner, inner):
            got = sum(
                nn(w[start : start + count, :], normed_ref[pl.ds(o, half), :])
                for w, o in zip(w_refs, offsets)
            ).astype(bf16)
            if start == 0:
                q_ref[...] = got
            else:
                kv_ref[start - inner : start - inner + count, :] = got

    normed_one, stats_one, queries, own_kv = call(
        first_kernel,
        [((width, rows), bf16), ((8, rows), f32), ((inner, rows), bf16), ((2 * inner, rows), bf16)],
        raw, columns, *in_parts, flops=6 * inner * width * rows, name="first",
    )

    def allowed_pairs(key_ref, query_ref):
        key_at = lax.broadcasted_iota(jnp.int32, (span, rows), 0)
        query_at = lax.broadcasted_iota(jnp.int32, (span, rows), 1) + before_rows
        return (key_at <= query_at) & (key_ref[...] == query_ref[...])

    def live_scale(head):
        return jnp.where(lax.axis_index("tp") * heads_local + head < HEADS, 1.0, 0.0).astype(f32)

    def attend_kernel(key_ref, query_ref, col_ref, q_ref, kv_ref, *refs):
        x_refs, w_refs = refs[:back], refs[back : back + n_parts]
        normed_ref, k_ref, v_ref, att_ref, log_ref = refs[back + n_parts :]
        offsets = half_offsets(paired, half)
        for i, x_ref in enumerate(x_refs):
            lanes = slice(i * rows, (i + 1) * rows)
            value = x_ref[...].astype(f32)
            mean, inverse = norm_stats(value)
            normed = (value - mean) * inverse * col_ref[:, 0:1] + col_ref[:, 1:2]
            normed_ref[:, lanes] = normed.astype(bf16)
            for out_ref, start in ((k_ref, inner), (v_ref, 2 * inner)):
                out_ref[:, lanes] = sum(
                    nn(w[start : start + inner, :], normed_ref[pl.ds(o, half), lanes])
                    for w, o in zip(w_refs, offsets)
                ).astype(bf16)
        k_ref[:, before_rows:] = kv_ref[:inner, :]
        v_ref[:, before_rows:] = kv_ref[inner:, :]
        allowed = allowed_pairs(key_ref, query_ref)
        for head in range(heads_local):
            at = slice(head * HEAD, (head + 1) * HEAD)
            scores = jnp.where(allowed, tn(k_ref[at, :], q_ref[at, :]) * score_scale, NEGATIVE)
            row_max = jnp.max(scores, axis=0, keepdims=True)
            piece = jnp.where(allowed, jnp.exp(scores - row_max), 0.0)
            row_sum = jnp.sum(piece, axis=0, keepdims=True)
            log_ref[head : head + 1, :] = row_max + jnp.log(row_sum)
            low = (piece * (1.0 / row_sum)).astype(bf16)
            att_ref[at, :] = (nn(v_ref[at, :], low) * live_scale(head)).astype(bf16)

    normed_before, keys, values, attended, log_total = call(
        attend_kernel,
        [
            ((width, before_rows), bf16), ((inner, span), bf16), ((inner, span), bf16),
            ((inner, rows), bf16), ((8 * (-(-heads_local // 8)), rows), f32),
        ],
        key_labels, query_labels, columns, queries, own_kv, *raw_blocks, *in_parts,
        flops=4 * inner * width * before_rows + 4 * inner * span * rows, name="attend",
    )

    def act_kernel(up_ref, *refs):
        out_ref = refs[-1]
        offsets = half_offsets(paired, half)
        for start, count in tiles(hidden, 256):
            out_ref[start : start + count, :] = sum(
                tn(w[:, start : start + count], up_ref[pl.ds(o, half), :])
                for w, o in zip(refs[:-1], offsets)
            )

    (act_gradient,) = call(
        act_kernel, [((hidden, rows), f32)], upstream, *down_parts,
        flops=2 * hidden * width * rows, name="act",
    )
    attended_pieces = [piece for _, piece in tp_gather(attended)]
    *out_rows, act_gradient, attended_late = lax.optimization_barrier(
        (*out_rows, act_gradient, attended)
    )
    out_other = [gather_parts(piece, 1) for piece in out_rows]
    out_pieces = [part for parts in out_other for part in parts]

    def middle_kernel(x_ref, col_ref, ag_ref, *refs):
        att_refs, refs = refs[:tp_size], refs[tp_size:]
        out_refs, refs = refs[: tp_size * n_parts], refs[tp_size * n_parts :]
        up_refs, refs = refs[:n_parts], refs[n_parts:]
        res_ref, stats_ref, normed_ref, act_ref, bg_ref, *chunk_refs = refs[: 5 + tp_size]
        part_ref = refs[5 + tp_size]
        offsets = half_offsets(paired, half)
        for p, o in enumerate(offsets):
            total = x_ref[pl.ds(o, half), :].astype(f32)
            for i, att in enumerate(att_refs):
                total = total + tn(out_refs[i * n_parts + p][...], att[...])
            res_ref[pl.ds(o, half), :] = total
        value = res_ref[...]
        mean, inverse = norm_stats(value)
        put_rows(stats_ref, [mean, inverse])
        normed = (value - mean) * inverse * col_ref[:, 2:3] + col_ref[:, 3:4]
        normed_ref[...] = normed.astype(bf16)
        for start, count in tiles(hidden, 256):
            at = slice(start, start + count)
            before = sum(
                tn(w[:, at], normed_ref[pl.ds(o, half), :]) for w, o in zip(up_refs, offsets)
            )
            value, slope = gelu_parts(before)
            act_ref[at, :] = value.astype(bf16)
            bg_ref[at, :] = (slope * ag_ref[at, :]).astype(bf16)
        for w, o in zip(up_refs, offsets):
            part_ref[pl.ds(o, half), :] = nn(w[...], bg_ref[...])
        spread_chunks(chunk_refs, part_ref, share, tp_size)

    residual, stats_two, normed_two, activated, before_gradient, own_chunk, *chunks = (
        pl.pallas_call(
            middle_kernel,
            out_shape=[
                jax.ShapeDtypeStruct((width, rows), f32),
                jax.ShapeDtypeStruct((8, rows), f32),
                jax.ShapeDtypeStruct((width, rows), bf16),
                jax.ShapeDtypeStruct((hidden, rows), bf16),
                jax.ShapeDtypeStruct((hidden, rows), bf16),
            ]
            + [jax.ShapeDtypeStruct((share, rows), bf16)] * tp_size,
            scratch_shapes=[pltpu.VMEM((width, rows), f32)],
            compiler_params=pltpu.CompilerParams(vmem_limit_bytes=40 << 20),
            name="middle",
        )(raw, columns, act_gradient, *attended_pieces, *out_pieces, *up_parts)
    )
    received = tp_send(chunks)

    def down_kernel(act_ref, *refs):
        w_refs, chunk_refs, part_ref = refs[:n_parts], refs[n_parts:-1], refs[-1]
        for w, o in zip(w_refs, half_offsets(paired, half)):
            part_ref[pl.ds(o, half), :] = nn(w[...], act_ref[...])
        spread_chunks(chunk_refs, part_ref, share, tp_size)

    own_forward, *forward_chunks = pl.pallas_call(
        down_kernel,
        out_shape=[jax.ShapeDtypeStruct((share, rows), bf16)] * tp_size,
        scratch_shapes=[pltpu.VMEM((width, rows), f32)],
        compiler_params=pltpu.CompilerParams(vmem_limit_bytes=36 << 20),
        cost_estimate=pl.CostEstimate(
            flops=2 * hidden * width * rows, bytes_accessed=4 << 20, transcendentals=0
        ),
        name="down",
    )(activated, *down_parts)

    def own_model(model):
        if not paired:
            return [model]
        return [
            take_rows(model, own_at, half), swap(take_rows(model, half - own_at, half))
        ]

    def both(array):
        return [array, swap(array)] if paired else [array]

    def reduced(whole, axis):
        if paired:
            return whole
        return lax.psum_scatter(
            whole.astype(bf16), "fsdp", scatter_dimension=axis, tiled=True
        ).astype(f32)

    def model_first(model, other):
        return reduced(sum(nt(m, o) for m, o in zip(model, other)), 0).astype(bf16)

    def model_last(other, model):
        return reduced(sum(nt(o, m) for m, o in zip(model, other)), 1).astype(bf16)

    down_term = model_first(own_model(upstream), both(activated))
    up_term = model_first(own_model(normed_two), both(before_gradient))
    second_share = add_up(own_chunk, received).astype(bf16)
    second_share, down_term, up_term, own_forward = lax.optimization_barrier(
        (second_share, down_term, up_term, own_forward)
    )
    second_pieces = [piece for _, piece in tp_gather(second_share)]
    down_gradient, up_gradient = ctx_sum_pair(down_term, up_term)

    def back_kernel(
        key_ref, query_ref, col_ref, up_ref, res_ref, stats_ref, q_ref, k_ref, v_ref, att_ref,
        log_ref, *refs
    ):
        dn_refs, refs = refs[:tp_size], refs[tp_size:]
        out_refs, refs = refs[:n_parts], refs[n_parts:]
        low_ref, own_ref, vec_ref, dq_ref, *rest = refs
        d_refs, (full_ref, da_ref) = rest[: back + 1], rest[back + 1 :]
        at = lax.axis_index("tp")
        for k, ref in enumerate(dn_refs):
            start = aligned(lax.rem(at + tp_size - k, tp_size) * share)
            full_ref[pl.ds(start, share), :] = ref[...].astype(f32)
        upstream_two = full_ref[...]
        mean, inverse = stats_ref[0:1, :], stats_ref[1:2, :]
        scaled = (res_ref[...] - mean) * inverse
        ones = jnp.ones((8, rows), f32)
        for i, value in enumerate((upstream_two * scaled, upstream_two)):
            vec_ref[i : i + 1, :] = lax.dot_general(
                ones, value, (((1,), (1,)), ((), ())),
                precision=lax.Precision.HIGHEST, preferred_element_type=f32,
            )[0:1, :]
        weighted = upstream_two * col_ref[:, 2:3]
        first = jnp.mean(weighted, axis=0, keepdims=True)
        second = jnp.mean(weighted * scaled, axis=0, keepdims=True)
        gradient = up_ref[...].astype(f32) + inverse * (weighted - first - scaled * second)
        full_ref[...] = gradient
        low_ref[...] = gradient.astype(bf16)
        own_ref[...] = full_ref[pl.ds(aligned(at * share), share), :]
        da = sum(
            nn(w[...], low_ref[pl.ds(o, half), :])
            for w, o in zip(out_refs, half_offsets(paired, half))
        )
        allowed = allowed_pairs(key_ref, query_ref)
        for head in range(heads_local):
            hs = slice(head * HEAD, (head + 1) * HEAD)
            da_low = (da[hs, :] * live_scale(head)).astype(bf16)
            delta = jnp.sum(
                da_low.astype(f32) * att_ref[hs, :].astype(f32), axis=0, keepdims=True
            )
            scores = tn(k_ref[hs, :], q_ref[hs, :]) * score_scale
            weights = jnp.where(allowed, jnp.exp(scores - log_ref[head : head + 1, :]), 0.0)
            score_gradient = (weights * (tn(v_ref[hs, :], da_low) - delta)).astype(bf16)
            dq_ref[hs, :] = (nn(k_ref[hs, :], score_gradient) * score_scale).astype(bf16)
            dk = (nt(q_ref[hs, :], score_gradient) * score_scale).astype(bf16)
            dv = nt(da_low, weights.astype(bf16)).astype(bf16)
            vs = slice(inner + head * HEAD, inner + (head + 1) * HEAD)
            for i, d_ref in enumerate(d_refs):
                lanes = slice(i * rows, (i + 1) * rows)
                d_ref[hs, :] = dk[:, lanes]
                d_ref[vs, :] = dv[:, lanes]

    residual_low, residual_own, second_sums, query_gradient, *block_terms = pl.pallas_call(
        back_kernel,
        out_shape=[
            jax.ShapeDtypeStruct((width, rows), bf16),
            jax.ShapeDtypeStruct((share, rows), f32),
            jax.ShapeDtypeStruct((8, width), f32),
            jax.ShapeDtypeStruct((inner, rows), bf16),
        ]
        + [jax.ShapeDtypeStruct((2 * inner, rows), bf16)] * (back + 1),
        scratch_shapes=[pltpu.VMEM((width, rows), f32), pltpu.VMEM((inner, rows), f32)],
        compiler_params=pltpu.CompilerParams(vmem_limit_bytes=40 << 20),
        name="back",
    )(
        key_labels, query_labels, columns, upstream, residual, stats_two, queries, keys, values,
        attended, log_total, *second_pieces, *out_pieces[:n_parts],
    )
    received_terms = [
        lax.ppermute(block_terms[back - k], "ctx", [(i + k, i) for i in range(ctx_size - k)])
        for k in range(1, back + 1)
    ]

    out_gradient = model_last(both(attended), own_model(residual_low))
    own_one, own_before = own_model(normed_one), own_model(normed_before)
    query_in = model_last(both(query_gradient), own_one)
    terms = [both(term) for term in block_terms]
    lefts = [jnp.concatenate([t[i] for t in terms], 1) for i in range(len(own_one))]
    rights = [jnp.concatenate([b, o], 1) for b, o in zip(own_before, own_one)]
    key_value_in = model_last(lefts, rights)
    first_half, second_half = ctx_sum_pair(
        jnp.concatenate([query_in, key_value_in[:inner]], 0),
        jnp.concatenate([key_value_in[inner:], out_gradient], 0),
    )
    in_gradient = jnp.concatenate([first_half, second_half[:inner]], 0).astype(f32)
    out_gradient = second_half[inner:].astype(f32)

    def last_kernel(x_ref, stats_ref, col_ref, dq_ref, own_ref, *refs):
        got_refs, refs = refs[:back], refs[back:]
        w_refs, refs = refs[:n_parts], refs[n_parts:]
        sums_ref, vec_ref, *chunk_refs = refs[: 2 + tp_size]
        part_ref, all_ref = refs[2 + tp_size :]
        all_ref[:inner, :] = dq_ref[...]
        all_ref[inner:, :] = sum(
            (got[...].astype(f32) for got in got_refs), own_ref[...].astype(f32)
        ).astype(bf16)
        for w, o in zip(w_refs, half_offsets(paired, half)):
            for start, count in tiles(half, 256):
                part_ref[pl.ds(o + start, count), :] = tn(w[:, start : start + count], all_ref[...])
        spread_chunks(chunk_refs, part_ref, share, tp_size)
        partial = part_ref[...]
        scaled = (x_ref[...].astype(f32) - stats_ref[0:1, :]) * stats_ref[1:2, :]
        product = partial * scaled
        gain = col_ref[:, 0:1]
        put_rows(
            sums_ref,
            [
                jnp.sum(partial * gain, axis=0, keepdims=True),
                jnp.sum(product * gain, axis=0, keepdims=True),
            ],
        )
        ones = jnp.ones((8, rows), f32)
        for i, value in enumerate((product, partial)):
            vec_ref[i : i + 1, :] = lax.dot_general(
                ones, value, (((1,), (1,)), ((), ())),
                precision=lax.Precision.HIGHEST, preferred_element_type=f32,
            )[0:1, :]

    stat_part, first_sums, own_first, *first_chunks = pl.pallas_call(
        last_kernel,
        out_shape=[
            jax.ShapeDtypeStruct((8, rows), f32),
            jax.ShapeDtypeStruct((8, width), f32),
        ]
        + [jax.ShapeDtypeStruct((share, rows), bf16)] * tp_size,
        scratch_shapes=[pltpu.VMEM((width, rows), f32), pltpu.VMEM((3 * inner, rows), bf16)],
        compiler_params=pltpu.CompilerParams(vmem_limit_bytes=36 << 20),
        name="last",
    )(raw, stats_one, columns, query_gradient, block_terms[back], *received_terms, *in_parts)

    def half_sums(sums):
        if paired:
            own = lax.dynamic_slice_in_dim(sums[:2], own_at, half, 1)
            return own + swap(lax.dynamic_slice_in_dim(sums[:2], half - own_at, half, 1))
        return lax.psum_scatter(sums[:2], "fsdp", scatter_dimension=1, tiled=True)

    received_first = tp_send(first_chunks)
    sums = tp_sum(jnp.concatenate([stat_part[:2], half_sums(first_sums)], 1))
    first_share = add_up(own_first, received_first)
    own_forward, stat_ready = lax.optimization_barrier((own_forward, stat_part))
    forward_chunks, _ = lax.optimization_barrier((forward_chunks, stat_ready))
    output_share = take_rows(residual, share_at, share) + add_up(
        own_forward, tp_send(forward_chunks)
    )
    own_scaled = (take_rows(raw, share_at, share).astype(f32) - stats_one[0:1]) * stats_one[1:2]
    own_gain = take_rows(columns, share_at, share)[:, 0:1]
    inputs_share = residual_own + stats_one[1:2] * (
        first_share * own_gain - sums[0:1, :rows] / width - own_scaled * (sums[1:2, :rows] / width)
    )
    vectors = ctx_sum_small(jnp.concatenate([sums[:, rows:], half_sums(second_sums)], 0))

    def share_out(array):
        return array.T.reshape(seqs_local, rows, share)

    return (
        share_out(output_share),
        share_out(inputs_share),
        in_gradient.reshape(3, inner, -1).transpose(2, 0, 1),
        out_gradient,
        up_gradient.astype(f32),
        down_gradient.astype(f32).T,
        vectors[0],
        vectors[1],
        vectors[2],
        vectors[3],
    )


def solution(mesh):
    placed = (
        P("fsdp", "ctx", None),
        P("fsdp", None),
        P("fsdp", None, "tp"),
        P("tp", "fsdp"),
        P("fsdp", "tp"),
        P("tp", "fsdp"),
        P("fsdp"),
        P("fsdp"),
        P("fsdp"),
        P("fsdp"),
        P("fsdp", "ctx", None),
    )
    return jax.shard_map(
        on_device,
        mesh=mesh,
        in_specs=placed,
        out_specs=(
            P("fsdp", "ctx", "tp"),
            P("fsdp", "ctx", "tp"),
            P("fsdp", None, "tp"),
            P("tp", "fsdp"),
            P("fsdp", "tp"),
            P("tp", "fsdp"),
            P("fsdp"),
            P("fsdp"),
            P("fsdp"),
            P("fsdp"),
        ),
        check_vma=False,
    )
```
